32 devices in a mesh: tm: 8 (over y, x, core), lane: 4 (over z).
Axes of the slice: x: 2, y: 2, z: 4, core: 2. Of those that a mesh axis runs over, the one named last changes fastest.
Arguments:
- replay: bfloat16 [4, 8, 1024, 1024], P('lane', 'tm'), may hold values from -6 to 6
- block_owner: int32 [8, 4, 8, 1], P('tm'), may hold values from 0 to 3; in each aligned block of 8 rows (0 to 7, 8 to 15, ..., all dimensions but the last counted through in order) at most 2 rows name the same one
- block_slot: int32 [8, 4, 8], P('tm'), may hold values from 0 to 3
- block_fill: int32 [4, 8, 8], P('lane', 'tm'), may hold values from 64 to 256
- log_decay: float32 [4, 16, 16384], P('lane', None, 'tm'), may hold values from -2 to 0
- resets: int32 [4, 16384], P('lane', 'tm'), may hold values from 0 to 1, as said below
- cotangent: bfloat16 [4, 16384, 1024], P('lane', 'tm'), may hold values from -6 to 6
- w_in: bfloat16 [1024, 1024], replicated, may hold values from -0.1875 to 0.1875
- w_bc: bfloat16 [1024, 128], replicated, may hold values from -0.01171875 to 0.01171875
- w_out: bfloat16 [1024, 1024], replicated, may hold values from -0.1875 to 0.1875
Outputs:
- grad_in: float32 [1024, 1024], P(('tm', 'lane'))
- grad_bc: float32 [1024, 128], P(('tm', 'lane'))
- grad_out: float32 [1024, 1024], P(('tm', 'lane'))
The draws below stay inside these ranges and needn't reach their ends.
Inputs may be any that keep to these rules, and one draw needn't show every extreme that they name: `block_owner`: among the 8 blocks of one segment on one time shard, no owner is named more than 2 times. `resets`: exactly one step of each segment is flagged.
All inputs are finite; a program needn't handle non-finite values.
Results may differ from the reference program's by a relative error of at most 0.0057.
Values may be sent and summed in bfloat16 or wider, within the bound.
A program may use at most 192 MiB of HBM per device.

```python
import math
import jax
import jax.numpy as jnp
import numpy as np
from jax import lax

D = 1024
HEAD = 64
STATE = 64
BLOCK = 256
BUFCH = 4
TOK_DEV = 2048
HEADS = 16
BLOCKS = 8
SEGMENT_COUNT = 4
SHARDS = 8
SEGMENT_STEPS = 16384
ROWS = 65536
CAP = 2


def draw_log_decay(key, part):
    random_keys_split = jax.random.split(key, 6)
    keep_share = 0.5
    sluggish_heads = jax.random.uniform(random_keys_split[0], (SEGMENT_COUNT, HEADS, 1)) < keep_share
    slow_rate = jax.random.uniform(random_keys_split[1], (SEGMENT_COUNT, HEADS, 1), jnp.float32, 0.2, 1.0) / SEGMENT_STEPS
    fast_rate = jax.random.uniform(random_keys_split[2], (SEGMENT_COUNT, HEADS, 1), jnp.float32, 10.0, 17.0) / BLOCK
    baseline_rate = jnp.where(sluggish_heads, slow_rate, fast_rate)
    jaggedness_level = jnp.exp(jax.random.uniform(random_keys_split[3], (SEGMENT_COUNT, HEADS, SEGMENT_STEPS), jnp.float32, math.log(0.5), math.log(2.0)))
    spike_position = jax.random.randint(random_keys_split[4], (SEGMENT_COUNT, 2), 0, SEGMENT_STEPS)
    spike_strike = jnp.any(lax.broadcasted_iota(jnp.int32, (SEGMENT_COUNT, 2, SEGMENT_STEPS), 2) == spike_position[:, :, None], axis=1)
    spike_penalty = jnp.log(jax.random.uniform(random_keys_split[5], (SEGMENT_COUNT, 1, SEGMENT_STEPS), jnp.float32, 0.6, 0.8))
    spike_decline = jnp.where(spike_strike[:, None, :] & sluggish_heads, spike_penalty, 0.0)
    return -baseline_rate * jaggedness_level + spike_decline


def draw_resets(key, part):
    reset_at = jax.random.randint(key, (SEGMENT_COUNT,), 1, SEGMENT_STEPS)
    return (lax.broadcasted_iota(jnp.int32, (SEGMENT_COUNT, SEGMENT_STEPS), 1) == reset_at[:, None]).astype(jnp.int32)


def place_ends(array, rng, least, high):
    longest = array.shape.index(max(array.shape))
    spots = []
    for shift in (0, 1):
        where = [jax.random.randint(jax.random.fold_in(rng, axis), (), 0, length) for axis, length in enumerate(array.shape)]
        where[longest] = (where[longest] + shift) % array.shape[longest]
        spots.append(tuple(where))
    return array.at[spots[0]].set(least).at[spots[1]].set(high)


def shard_levels(stream_key, dims, pieces, low, largest):
    level = 1.0
    for dim, shards_of in pieces:
        draws = jax.random.uniform(jax.random.fold_in(jax.random.fold_in(stream_key, 6), dim), (shards_of,), jnp.float32, low / len(pieces), largest / len(pieces))
        level = level * jnp.repeat(jnp.exp(draws), dims[dim] // shards_of).reshape((-1,) + (1,) * (len(dims) - 1 - dim))
    return level


def shared_out(key, own, number, rows, number_of, top, bound, skew):
    ranking = jax.random.permutation(key, number_of)
    heavy_load, usual = portions_of(number_of, rows * top, bound, skew, True), portions_of(number_of, rows * top, bound, skew, False)
    places = jnp.arange(number_of)

    def named(sizes, turn):
        used = int((sizes > 0).sum())
        fixed = max(1, used // 4)
        passed = fixed + (places - fixed + turn * (used - fixed)) % max(1, number_of - fixed)
        return jnp.zeros((number_of,), jnp.int32).at[ranking[jnp.where(places < fixed, places, passed)]].set(jnp.asarray(sizes, jnp.int32))

    sizes = jnp.where(number % 4 == 0, named(heavy_load, number // 4), named(usual, number - number // 4 - 1))
    mixed = jax.random.permutation(jax.random.fold_in(own, 3), number_of)
    giver, taker = mixed[0:number_of // 2 * 2:2], mixed[1:number_of // 2 * 2:2]
    margin = jnp.minimum(sizes[giver] - 1, bound - sizes[taker]) // 2
    margin = jnp.where((giver == ranking[0]) | (taker == ranking[0]) | (sizes[taker] == 0), 0, jnp.maximum(margin, 0))
    passed = jax.random.randint(jax.random.fold_in(own, 4), (number_of // 2,), 0, 1 << 20) % (margin + 1)
    sizes = sizes.at[giver].add(-passed).at[taker].add(passed)
    items = jnp.searchsorted(jnp.cumsum(sizes), jnp.arange(rows * top), side="right").astype(jnp.int32)
    grid = items.reshape(top, rows).T
    grid = grid[jax.random.permutation(jax.random.fold_in(own, 1), rows)]
    turn = jax.random.randint(jax.random.fold_in(own, 2), (rows, 1), 0, top)
    return jnp.take_along_axis(grid, (jnp.arange(top)[None, :] + turn) % top, axis=1)


def portions_of(amount, total, bound, lean, full):
    weights = [(1 << 20) // math.isqrt(standing ** lean) + 1 for standing in range(1, amount + 1)]
    largest = bound if full else min(bound, max(-(-total // amount), total * weights[0] // sum(weights)))
    least = 1 if total - largest >= amount - 1 else 0
    counts, spare = [largest] + [least] * (amount - 1), total - largest - least * (amount - 1)
    while spare > 0:
        movable = [i for i in range(1, amount) if counts[i] < largest] or [i for i in range(1, amount) if counts[i] < bound]
        whole, left = sum([weights[i] for i in movable]), spare
        for i in movable:
            more = min(bound - counts[i], max(1, left * weights[i] // whole), spare)
            counts[i] = counts[i] + more
            spare = spare - more
    return np.array(counts)


def normal_values(own_key, dims, scale, bound, cuts=(), kind=jnp.bfloat16):
    values = jax.random.normal(own_key, dims, jnp.float32) * scale
    if len(cuts) > 0:
        values = shard_levels(own_key, dims, cuts, -0.22, 0.18) * values
    return jnp.clip(values, min=-bound, max=bound).astype(kind)


def setup_inputs(seed: int = 0) -> dict:
    streams_of = jax.random.split(jax.random.key(seed), 11)
    replay = normal_values(streams_of[0], (SEGMENT_COUNT, SHARDS, BUFCH * BLOCK, D), 1.0, 6.0, ((0, 4), (1, 8)))
    block_owner_keys = jax.random.split(jax.random.fold_in(streams_of[1], 1), SHARDS * SEGMENT_COUNT * BLOCKS // BLOCKS)
    block_owner_turns = jax.random.permutation(jax.random.fold_in(streams_of[1], 3), SHARDS * SEGMENT_COUNT * BLOCKS // BLOCKS)
    block_owner = jax.vmap(lambda own, number: shared_out(jax.random.fold_in(streams_of[1], 2), own, number, BLOCKS, SEGMENT_COUNT, 1, CAP, 2))(block_owner_keys, block_owner_turns).reshape((SHARDS, SEGMENT_COUNT, BLOCKS, 1))
    block_slot = place_ends(jax.random.randint(streams_of[2], (SHARDS, SEGMENT_COUNT, BLOCKS), 0, BUFCH), jax.random.fold_in(streams_of[2], 1), 0, BUFCH - 1).astype(jnp.int32)
    block_fill = place_ends(jax.random.randint(streams_of[3], (SEGMENT_COUNT, SHARDS, BLOCKS), BLOCK // 4, BLOCK + 1), jax.random.fold_in(streams_of[3], 1), BLOCK // 4, BLOCK).astype(jnp.int32)
    log_decay = draw_log_decay(jax.random.fold_in(streams_of[10], 71), 0)
    resets = draw_resets(jax.random.fold_in(streams_of[10], 71), 0)
    cotangent = normal_values(streams_of[6], (SEGMENT_COUNT, SEGMENT_STEPS, D), 1.0, 6.0, ((0, 4), (1, 8)))
    w_in = normal_values(streams_of[7], (D, D), D ** -0.5, 0.1875)
    w_bc = normal_values(streams_of[8], (D, 2 * STATE), (4 * D * STATE) ** -0.5, 0.01171875)
    w_out = normal_values(streams_of[9], (D, D), D ** -0.5, 0.1875)
    return {"replay": replay, "block_owner": block_owner, "block_slot": block_slot, "block_fill": block_fill, "log_decay": log_decay, "resets": resets, "cotangent": cotangent, "w_in": w_in, "w_bc": w_bc, "w_out": w_out}


def decay_matrix(log_rate, episode_flags):
    cumulated = jnp.cumsum(log_rate, axis=1)
    counted = jnp.cumsum(episode_flags)
    extent = log_rate.shape[1]
    row_pos = lax.broadcasted_iota(jnp.int32, (extent, extent), 0)
    col_pos = lax.broadcasted_iota(jnp.int32, (extent, extent), 1)
    linked = (counted[:, None] == counted[None, :]) & (col_pos <= row_pos)
    spread = jnp.where(linked[None], cumulated[:, :, None] - cumulated[:, None, :], 0.0)
    return jnp.where(linked[None], jnp.exp(spread), 0.0)

def edge_weights(log_rate, episode_flags):
    cumulated = jnp.cumsum(log_rate, axis=1)
    counted = jnp.cumsum(episode_flags)
    opening = jnp.where(counted[None, :] == 0, jnp.exp(cumulated), 0.0)
    closing = jnp.where(counted[None, :] == counted[-1], jnp.exp(cumulated[:, -1:] - cumulated), 0.0)
    return (opening, closing)

def product(spec, left_op, right_op):
    return jnp.einsum(spec, left_op.astype(jnp.float32), right_op.astype(jnp.float32))

def block_grads(block_items):
    inner_proj, write_keys, read_keys, upstream, log_rate, episode_flags, opening, closing, weighted_in, weighted_out, start_state, end_adjoint = block_items
    extent = inner_proj.shape[0]
    decays = decay_matrix(log_rate, episode_flags)
    scores = jnp.dot(read_keys, write_keys.T, preferred_element_type=jnp.float32)
    mixing = (decays * scores[None]).astype(jnp.bfloat16)
    state_bf = start_state.astype(jnp.bfloat16)
    adjoint_bf = end_adjoint.astype(jnp.bfloat16)
    carried = product('in,hpn->ihp', read_keys, state_bf)
    readout = product('hij,jhp->ihp', mixing, inner_proj) + opening.T[:, :, None] * carried
    pairing = product('ihp,jhp->hij', upstream, inner_proj)
    blended = (decays * pairing).astype(jnp.bfloat16)
    returned = product('jn,hpn->jhp', write_keys, adjoint_bf)
    grad_inner = product('hij,ihp->jhp', mixing, upstream) + closing.T[:, :, None] * returned
    grad_write = product('hij,in->jn', blended, read_keys) + product('jhp,hpn->jn', weighted_in, adjoint_bf)
    grad_read = product('hij,jn->in', blended, write_keys) + product('ihp,hpn->in', weighted_out, state_bf)
    return (readout.astype(jnp.bfloat16).reshape(extent, -1), grad_inner.astype(jnp.bfloat16).reshape(extent, -1), jnp.concatenate([grad_write, grad_read], axis=1).astype(jnp.bfloat16))

def advance(carried_in, block_items):
    current, gained = carried_in
    block_factor, pushed = block_items
    return ((block_factor[:, None, None] * current + pushed, gained * block_factor), (current, gained))

def reference(replay, block_owner, block_slot, block_fill, log_decay, resets, cotangent, w_in, w_bc, w_out):
    num_heads = D // HEAD
    stacked = replay.reshape(SEGMENT_COUNT, SHARDS, BUFCH, BLOCK, D)
    owners = block_owner[..., 0].astype(jnp.int32)
    shard_ids = lax.broadcasted_iota(jnp.int32, owners.shape, 0)
    taken = stacked[owners, shard_ids, block_slot.astype(jnp.int32)]
    delivered_all = jnp.transpose(taken, (1, 0, 2, 3, 4)).reshape(SEGMENT_COUNT, SEGMENT_STEPS, D)
    usable = (lax.broadcasted_iota(jnp.int32, (SEGMENT_COUNT, SHARDS, TOK_DEV // BLOCK, BLOCK), 3) < block_fill[..., None]).reshape(SEGMENT_COUNT, SEGMENT_STEPS)
    delivered_all = jnp.where(usable[..., None], delivered_all, jnp.zeros((), delivered_all.dtype))
    masked_all = jnp.where(usable[..., None], cotangent, jnp.zeros((), cotangent.dtype))
    block_total = SEGMENT_STEPS // BLOCK

    def per_lane(summed, lane_items):
        delivered, masked, rates, episode_flags = lane_items
        inner_proj = jnp.dot(delivered, w_in, preferred_element_type=jnp.float32).astype(jnp.bfloat16)
        projected = jnp.dot(delivered, w_bc, preferred_element_type=jnp.float32).astype(jnp.bfloat16)
        upstream = jnp.dot(masked, w_out.T, preferred_element_type=jnp.float32).astype(jnp.bfloat16)
        inner_b = inner_proj.reshape(block_total, BLOCK, num_heads, HEAD)
        upstream_b = upstream.reshape(block_total, BLOCK, num_heads, HEAD)
        write_b = projected[:, :STATE].reshape(block_total, BLOCK, STATE)
        read_b = projected[:, STATE:].reshape(block_total, BLOCK, STATE)
        rates_b = jnp.transpose(rates.reshape(num_heads, block_total, BLOCK), (1, 0, 2))
        flags_b = episode_flags.reshape(block_total, BLOCK)
        opening, closing = jax.vmap(edge_weights)(rates_b, flags_b)
        factor = opening[:, :, -1]
        weighted_in = (jnp.transpose(closing, (0, 2, 1))[..., None] * inner_b).astype(jnp.bfloat16)
        weighted_out = (jnp.transpose(opening, (0, 2, 1))[..., None] * upstream_b).astype(jnp.bfloat16)
        push_fwd = product('kjhp,kjn->khpn', weighted_in, write_b)
        push_bwd = product('kihp,kin->khpn', weighted_out, read_b)
        zero_state = jnp.zeros((num_heads, HEAD, STATE), jnp.float32)
        unit_gain = jnp.ones((num_heads,), jnp.float32)
        starts = lax.scan(advance, (zero_state, unit_gain), (factor, push_fwd))[1][0]
        ends = lax.scan(advance, (zero_state, unit_gain), (factor, push_bwd), reverse=True)[1][0]
        readout, grad_inner, grad_keys = lax.map(block_grads, (inner_b, write_b, read_b, upstream_b, rates_b, flags_b, opening, closing, weighted_in, weighted_out, starts, ends))
        readout = readout.reshape(SEGMENT_STEPS, D)
        grad_inner = grad_inner.reshape(SEGMENT_STEPS, D)
        grad_keys = grad_keys.reshape(SEGMENT_STEPS, 2 * STATE)
        terms = jnp.concatenate([jnp.dot(delivered.T, grad_inner, preferred_element_type=jnp.float32), jnp.dot(delivered.T, grad_keys, preferred_element_type=jnp.float32), jnp.dot(readout.T, masked, preferred_element_type=jnp.float32)], axis=1)
        return (summed + terms, None)
    initial = jnp.zeros((D, 2 * D + 2 * STATE), jnp.float32)
    summed = lax.scan(per_lane, initial, (delivered_all, masked_all, log_decay, resets))[0]
    summed = summed * (1.0 / math.sqrt(ROWS))
    return (summed[:, :D], summed[:, D:D + 2 * STATE], summed[:, D + 2 * STATE:])
```

```python
import math

import jax
import jax.numpy as jnp
from jax import lax
from jax.experimental import pallas as pl
from jax.experimental.pallas import tpu as pltpu
from jax.sharding import PartitionSpec as P

STATE = 64
BLOCK = 256
BUFCH = 4
F32 = jnp.float32
BF = jnp.bfloat16


def dot(a, b, ca, cb):
    return lax.dot_general(a, b, (((ca,), (cb,)), ((), ())), preferred_element_type=F32)


def split3(x):
    hi = x.astype(BF)
    rest = x - hi.astype(F32)
    mid = rest.astype(BF)
    low = (rest - mid.astype(F32)).astype(BF)
    return hi, mid, low


def decay_parts(rates, heads):
    a = lax.broadcasted_iota(jnp.int32, (BLOCK, BLOCK), 0)
    b = lax.broadcasted_iota(jnp.int32, (BLOCK, BLOCK), 1)
    lower = (b <= a).astype(F32).astype(BF)
    cum_col = 0.0
    cum_row = 0.0
    for part in split3(rates):
        cum_col = cum_col + dot(lower, part, 1, 1)
        cum_row = cum_row + dot(part, lower, 1, 1)
    cnt_col = cum_col[:, heads : heads + 1]
    cnt_row = cum_row[heads : heads + 1, :]
    cum = cum_col[:, :heads]
    last = cum_col[BLOCK - 1 : BLOCK, :]
    opening = jnp.where(cnt_col == 0.0, jnp.exp(cum), 0.0)
    closing = jnp.where(
        cnt_col == last[:, heads : heads + 1], jnp.exp(last[:, :heads] - cum), 0.0
    )
    linked = (cnt_col == cnt_row) & (b <= a)
    return cum, cum_row, opening, closing, linked


def widen(x, heads, width):
    a = lax.broadcasted_iota(jnp.int32, (heads, width), 0)
    b = lax.broadcasted_iota(jnp.int32, (heads, width), 1)
    per = width // heads
    spread = ((b >= a * per) & (b < (a + 1) * per)).astype(F32).astype(BF)
    total = 0.0
    for part in split3(x):
        total = total + dot(part, spread, 1, 0)
    return total


def pick_kernel(sel, src, out):
    out[...] = src[...]


def project_kernel(
    heads,
    pick,
    fill,
    recv,
    up,
    rates,
    w_in,
    w_bc,
    rows_o,
    inner_o,
    keys_o,
    push_f,
    push_b,
    fac,
):
    k = pl.program_id(0)
    pos = lax.broadcasted_iota(jnp.int32, recv.shape[1:], 0)
    rows = jnp.where(pos < fill[k], recv[0], jnp.zeros((), BF))
    rows_o[...] = rows
    inner = dot(rows, w_in[...], 1, 0).astype(BF)
    inner_o[...] = inner
    keys = dot(rows, w_bc[...], 1, 0).astype(BF)
    keys_o[...] = keys
    _, _, opening, closing, _ = decay_parts(rates[...], heads)
    width = inner.shape[1]
    open_w = widen(opening, heads, width)
    close_w = widen(closing, heads, width)
    w_inn = (close_w * inner.astype(F32)).astype(BF)
    w_out = (open_w * up[...].astype(F32)).astype(BF)
    push_f[0] = dot(keys, w_inn, 0, 0)[:STATE]
    push_b[0] = dot(keys, w_out, 0, 0)[STATE:]
    fac[0] = jnp.broadcast_to(open_w[BLOCK - 1 : BLOCK], fac.shape[1:])


def mix_kernel(heads, inner_r, up_r, keys_r, rates, st, fin, read_o, gin_o, gk_o, acc):
    inner = inner_r[...]
    up = up_r[...]
    keys = keys_r[...]
    width = inner.shape[1]
    per = width // heads
    write = keys[:, :STATE]
    read = keys[:, STATE:]
    cum, cum_row, opening, closing, linked = decay_parts(rates[...], heads)
    bias = jnp.where(linked, 0.0, -1e30)
    scores = dot(read, write, 1, 1)
    open_w = widen(opening, heads, width)
    close_w = widen(closing, heads, width)
    start = st[0]
    finish = fin[0]
    up_t = up.T
    lane = lax.broadcasted_iota(jnp.int32, (BLOCK, 2 * per), 1)
    first = lane < per
    zero = jnp.zeros((), BF)
    carried = open_w * dot(read, start, 1, 0)
    returned = close_w * dot(write, finish, 1, 0)
    for g in range(heads // 2):
        cols = slice(2 * g * per, 2 * (g + 1) * per)
        in_p = inner[:, cols]
        up_p = up[:, cols]
        outs = []
        backs = []
        for s in range(2):
            h = 2 * g + s
            decay = jnp.exp(cum[:, h : h + 1] - cum_row[h : h + 1, :] + bias)
            mixing = (decay * scores).astype(BF)
            pairing = dot(jnp.where(first == (s == 0), up_p, zero), in_p, 1, 1)
            if h == 0:
                acc[...] = decay * pairing
            else:
                acc[...] += decay * pairing
            outs.append(dot(mixing, in_p, 1, 0))
            backs.append(dot(up_t[h * per : (h + 1) * per], mixing, 1, 0))
        read_o[:, cols] = (jnp.where(first, outs[0], outs[1]) + carried[:, cols]).astype(BF)
        back = jnp.concatenate(backs, axis=0).T
        gin_o[:, cols] = (back + returned[:, cols]).astype(BF)
    blended = acc[...].astype(BF)
    w_inn = (close_w * inner.astype(F32)).astype(BF)
    w_out = (open_w * up.astype(F32)).astype(BF)
    gk_o[:, :STATE] = (dot(blended, read, 0, 0) + dot(w_inn, finish, 1, 1)).astype(BF)
    gk_o[:, STATE:] = (dot(blended, write, 1, 0) + dot(w_out, start, 1, 1)).astype(BF)


def on_device(
    replay, block_owner, block_slot, block_fill, log_decay, resets, cotangent, w_in, w_bc, w_out
):
    lane_count = lax.axis_size("lane")
    shards = lax.axis_size("tm")
    my_lane = lax.axis_index("lane")
    mine = lax.axis_index("tm")
    width = replay.shape[3]
    heads = log_decay.shape[1]
    blocks = block_fill.shape[2]
    tokens = cotangent.shape[1]
    owners = block_owner[0, :, :, 0]
    slot_map = block_slot[0]
    my_owner = lax.dynamic_index_in_dim(owners, my_lane, 0, keepdims=False)
    capacity = max(2, (blocks + lane_count - 1) // lane_count)
    order_pos = lax.broadcasted_iota(jnp.int32, (blocks, blocks), 0)
    other_pos = lax.broadcasted_iota(jnp.int32, (blocks, blocks), 1)
    ranking = jnp.sum(
        ((owners[:, :, None] == owners[:, None, :]) & (other_pos < order_pos)[None]).astype(
            jnp.int32
        ),
        axis=2,
    )
    slot_ids = lax.broadcasted_iota(jnp.int32, (lane_count, capacity, blocks), 1)
    picked = (owners[:, None, :] == my_lane) & (ranking[:, None, :] == slot_ids)
    chosen = jnp.sum(jnp.where(picked, slot_map[:, None, :], 0), axis=2).reshape(-1)
    slots = lane_count * capacity
    outgoing = pl.pallas_call(
        pick_kernel,
        name="pick",
        out_shape=jax.ShapeDtypeStruct((slots, BLOCK, width), BF),
        grid_spec=pltpu.PrefetchScalarGridSpec(
            num_scalar_prefetch=1,
            grid=(slots,),
            in_specs=[pl.BlockSpec((1, BLOCK, width), lambda i, s: (s[i], 0, 0))],
            out_specs=pl.BlockSpec((1, BLOCK, width), lambda i, s: (i, 0, 0)),
        ),
    )(chosen, replay.reshape(BUFCH, BLOCK, width))
    received = lax.all_to_all(outgoing, "lane", split_axis=0, concat_axis=0, tiled=True)
    my_rank = lax.dynamic_index_in_dim(ranking, my_lane, 0, keepdims=False)
    pick = my_owner * capacity + my_rank
    fill = block_fill[0, 0]
    usable = (lax.broadcasted_iota(jnp.int32, (blocks, BLOCK), 1) < fill[:, None]).reshape(tokens)
    masked = jnp.where(usable[:, None], cotangent[0], jnp.zeros((), BF))
    upstream = dot(masked, w_out, 1, 1).astype(BF)
    pad = (-(heads + 1)) % 8
    rates = jnp.concatenate(
        [log_decay[0], resets.astype(F32), jnp.zeros((pad, tokens), F32)], axis=0
    )
    rate_rows = heads + 1 + pad
    row_spec = pl.BlockSpec((BLOCK, width), lambda k, *s: (k, 0))
    key_spec = pl.BlockSpec((BLOCK, 2 * STATE), lambda k, *s: (k, 0))
    rate_spec = pl.BlockSpec((rate_rows, BLOCK), lambda k, *s: (0, k))
    state_spec = pl.BlockSpec((1, STATE, width), lambda k, *s: (k, 0, 0))
    row_shape = jax.ShapeDtypeStruct((tokens, width), BF)
    key_shape = jax.ShapeDtypeStruct((tokens, 2 * STATE), BF)
    state_shape = jax.ShapeDtypeStruct((blocks, STATE, width), F32)
    rows, inner, keys, push_f, push_b, fac = pl.pallas_call(
        lambda *a: project_kernel(heads, *a),
        name="project",
        out_shape=(
            row_shape,
            row_shape,
            key_shape,
            state_shape,
            state_shape,
            jax.ShapeDtypeStruct((blocks, 8, width), F32),
        ),
        grid_spec=pltpu.PrefetchScalarGridSpec(
            num_scalar_prefetch=2,
            grid=(blocks,),
            in_specs=[
                pl.BlockSpec((1, BLOCK, width), lambda k, p, f: (p[k], 0, 0)),
                row_spec,
                rate_spec,
                pl.BlockSpec((width, width), lambda k, *s: (0, 0)),
                pl.BlockSpec((width, 2 * STATE), lambda k, *s: (0, 0)),
            ],
            out_specs=(
                row_spec,
                row_spec,
                key_spec,
                state_spec,
                state_spec,
                pl.BlockSpec((1, 8, width), lambda k, *s: (k, 0, 0)),
            ),
        ),
    )(pick, fill, received, upstream, rates, w_in, w_bc)
    factor = fac[:, :1]

    def sweep(order, push):
        state = jnp.zeros((STATE, width), F32)
        gain = jnp.ones((1, width), F32)
        states = [None] * blocks
        gains = [None] * blocks
        for k in order:
            states[k], gains[k] = state, gain
            state = factor[k] * state + push[k]
            gain = gain * factor[k]
        return state, gain, states, gains

    fwd = sweep(range(blocks), push_f)
    bwd = sweep(range(blocks - 1, -1, -1), push_b)
    packet = jnp.concatenate([fwd[0], bwd[0], jnp.broadcast_to(fwd[1], (8, width))], axis=0)
    pieces = lax.all_gather(packet, "tm")
    enter = jnp.zeros((STATE, width), F32)
    adjoint = jnp.zeros((STATE, width), F32)
    for s in range(shards - 1):
        r = shards - 1 - s
        enter = jnp.where(
            s < mine, pieces[s, 2 * STATE : 2 * STATE + 1] * enter + pieces[s, :STATE], enter
        )
        adjoint = jnp.where(
            r > mine,
            pieces[r, 2 * STATE : 2 * STATE + 1] * adjoint + pieces[r, STATE : 2 * STATE],
            adjoint,
        )
    starts = jnp.stack([(a + b * enter).astype(BF) for a, b in zip(fwd[2], fwd[3])])
    ends = jnp.stack([(a + b * adjoint).astype(BF) for a, b in zip(bwd[2], bwd[3])])
    readout, grad_inner, grad_keys = pl.pallas_call(
        lambda *a: mix_kernel(heads, *a),
        name="mix",
        out_shape=(row_shape, row_shape, key_shape),
        grid=(blocks,),
        in_specs=[row_spec, row_spec, key_spec, rate_spec, state_spec, state_spec],
        out_specs=(row_spec, row_spec, key_spec),
        scratch_shapes=[pltpu.VMEM((BLOCK, BLOCK), F32)],
    )(inner, upstream, keys, rates, starts, ends)
    devices = shards * lane_count
    grad_scale = 1.0 / math.sqrt(tokens * devices)

    def collect(terms):
        part = lax.all_to_all(
            terms.astype(BF), ("tm", "lane"), split_axis=0, concat_axis=0, tiled=True
        )
        part = part.reshape(devices, part.shape[0] // devices, part.shape[1])
        return jnp.sum(part.astype(F32), axis=0) * grad_scale

    g_out = collect(dot(readout, masked, 0, 0))
    g_in = collect(
        jnp.concatenate([dot(rows, grad_inner, 0, 0), dot(rows, grad_keys, 0, 0)], axis=1)
    )
    return (g_in[:, :width], g_in[:, width:], g_out)


def solution(mesh):
    placed = (
        P("lane", "tm", None, None),
        P("tm", None, None, None),
        P("tm", None, None),
        P("lane", "tm", None),
        P("lane", None, "tm"),
        P("lane", "tm"),
        P("lane", "tm", None),
        P(),
        P(),
        P(),
    )
    return jax.shard_map(
        on_device,
        mesh=mesh,
        in_specs=placed,
        out_specs=(P(("tm", "lane"), None), P(("tm", "lane"), None), P(("tm", "lane"), None)),
        check_vma=False,
    )
```
